512 devices in a mesh: seq: 32 (over x, y), head: 16 (over z, core).
Axes of the slice: x: 4, y: 8, z: 8, core: 2. Of those that a mesh axis runs over, the one named last changes fastest.
Arguments:
- slab_query: bfloat16 [4096, 8192], P('seq', 'head'), may hold values from -6 to 6
- slab_key: bfloat16 [4096, 8192], P('seq', 'head'), may hold values from -6 to 6
- slab_value: bfloat16 [4096, 8192], P('seq', 'head'), may hold values from -6 to 6
- slab_levels: bfloat16 [6, 64, 4096], P(None, 'head', 'seq'), may hold values from 0.1 to 10
- norm_gain: bfloat16 [8192], P('head'), may hold values from 0.5 to 1.5
- user_query: bfloat16 [512, 64, 8192], P('seq', None, 'head'), may hold values from -6 to 6
- user_key: bfloat16 [512, 64, 8192], P('seq', None, 'head'), may hold values from -6 to 6
- user_value: bfloat16 [512, 64, 8192], P('seq', None, 'head'), may hold values from -6 to 6
- user_levels: bfloat16 [512, 6, 64, 64], P('seq', None, 'head'), may hold values from 0.1 to 10
- prefix_lengths: int32 [512], P('seq'), may hold values from 1 to 31, as said below
Outputs:
- slab_out: bfloat16 [4096, 8192], P('seq', 'head')
- user_out: bfloat16 [512, 64, 8192], P('seq', None, 'head')
The draws below stay inside these ranges and needn't reach their ends.
Inputs may be any that keep to these rules, and one draw needn't show every extreme that they name: `prefix_lengths`: the 16 users that lie on one index of seq have distinct prefix lengths; one prefix length is held by one user of every index of seq.
All inputs are finite; a program needn't handle non-finite values.
Results may differ from the reference program's by a relative error of at most 0.012.
Values may be sent and summed in bfloat16 or wider, within the bound.
A program may use at most 64 MiB of HBM per device.

```python
import math
import jax
import jax.numpy as jnp
from jax import lax

HEADS = 64
HD = 128
TOK_DEV = 128
SUF = 64
LEVELS = 6
TOKENS = 4096
USERS_DEV = 16
USERS = 512
N_SEQ = 32


def level_draw(key, array_shape, head_axis):
    head_total = array_shape[head_axis]
    head_frac = jnp.arange(head_total, dtype=jnp.float32) / max(head_total - 1, 1)
    head_rise = jnp.power(10.0, head_frac)
    broadcast_shape = [1] * len(array_shape)
    broadcast_shape[head_axis] = head_total
    head_rise = head_rise.reshape(broadcast_shape)
    magnitude = jnp.exp(jax.random.uniform(key, array_shape, jnp.float32, math.log(0.1), 0.0))
    return magnitude * head_rise


def draw_slab_levels(key, part):
    return level_draw(jax.random.fold_in(key, 3), (LEVELS, HEADS, TOKENS), 1).astype(jnp.bfloat16)


def draw_user_levels(key, part):
    return level_draw(jax.random.fold_in(key, 5), (USERS, LEVELS, HEADS, SUF), 2).astype(jnp.bfloat16)


def draw_prefix_lengths(key, part):
    shared_len = jax.random.randint(jax.random.fold_in(key, 7), (), 1, N_SEQ)
    first_dev = jax.random.randint(jax.random.fold_in(key, 9), (), 0, N_SEQ)
    second_dev = (first_dev + 1 + jax.random.randint(jax.random.fold_in(key, 13), (), 0, N_SEQ - 1)) % N_SEQ
    device_keys = jax.random.split(jax.random.fold_in(key, 11), N_SEQ)
    device_ids = jnp.arange(N_SEQ, dtype=jnp.int32)

    def device_draw(device_key, device_id):
        key_scores, key_order = jax.random.split(device_key)
        candidates = jnp.arange(1, N_SEQ, dtype=jnp.int32)
        ranking = jax.random.permutation(key_scores, N_SEQ - 1).astype(jnp.int32)
        ranking = jnp.where(candidates == shared_len, -3, ranking)
        ranking = jnp.where(jnp.logical_and(device_id == first_dev, candidates == 1), -2, ranking)
        ranking = jnp.where(jnp.logical_and(device_id == second_dev, candidates == N_SEQ - 1), -2, ranking)
        ordering = jnp.argsort(ranking, stable=True)
        picked = candidates[ordering[:USERS_DEV]]
        return jax.random.permutation(key_order, picked)
    drawn = jax.vmap(device_draw)(device_keys, device_ids)
    return drawn.reshape(USERS).astype(jnp.int32)


def block_scale(key, extent, pieces, smallest, top_value):
    gain = 1.0
    for dim, shards_of in pieces:
        draws = jax.random.uniform(jax.random.fold_in(jax.random.fold_in(key, 6), dim), (shards_of,), jnp.float32, smallest / len(pieces), top_value / len(pieces))
        gain = gain * jnp.repeat(jnp.exp(draws), extent[dim] // shards_of).reshape((-1,) + (1,) * (len(extent) - 1 - dim))
    return gain


def normal_values(stream_key, extent, scale, limit, cuts=(), kind=jnp.bfloat16):
    gain = block_scale(stream_key, extent, cuts, -0.22, 0.18) if cuts else 1.0
    array = jax.random.normal(stream_key, extent, jnp.float32) * scale * gain
    return jnp.minimum(jnp.maximum(array, -limit), limit).astype(kind)


def setup_inputs(seed: int = 0) -> dict:
    splits = jax.random.split(jax.random.key(seed), 11)
    return {
        "slab_query": normal_values(splits[0], (TOKENS, HEADS * HD), 1.0, 6.0, ((0, 32), (1, 16))),
        "slab_key": normal_values(splits[1], (TOKENS, HEADS * HD), 1.0, 6.0, ((0, 32), (1, 16))),
        "slab_value": normal_values(splits[2], (TOKENS, HEADS * HD), 1.0, 6.0, ((0, 32), (1, 16))),
        "slab_levels": draw_slab_levels(jax.random.fold_in(splits[10], 71), 0),
        "norm_gain": jnp.clip(1.0 + 0.1 * jax.random.normal(splits[4], (HEADS * HD,), jnp.float32), 0.5, 1.5).astype(jnp.bfloat16),
        "user_query": normal_values(splits[5], (USERS, SUF, HEADS * HD), 1.0, 6.0, ((0, 32), (2, 16))),
        "user_key": normal_values(splits[6], (USERS, SUF, HEADS * HD), 1.0, 6.0, ((0, 32), (2, 16))),
        "user_value": normal_values(splits[7], (USERS, SUF, HEADS * HD), 1.0, 6.0, ((0, 32), (2, 16))),
        "user_levels": draw_user_levels(jax.random.fold_in(splits[10], 71), 0),
        "prefix_lengths": draw_prefix_lengths(jax.random.fold_in(splits[10], 71), 0),
    }


def local_part(query_rows, key_rows, value_rows, first_weights):
    scores = jnp.einsum('bthd,bshd->bhts', query_rows.astype(jnp.float32), key_rows.astype(jnp.float32))
    token_count = query_rows.shape[1]
    causal_mask = jnp.arange(token_count)[:, None] >= jnp.arange(token_count)[None, :]
    scores = jnp.where(causal_mask, scores, jnp.zeros_like(scores)).astype(jnp.bfloat16)
    result = jnp.einsum('bhts,bshd->bthd', scores.astype(jnp.float32), value_rows.astype(jnp.float32))
    return result * jnp.transpose(first_weights, (0, 2, 1)).astype(jnp.float32)[..., None]

def read_prefix(query_rows, level_weights, node_states):
    level_count, head_count, inner, outer = node_states.shape
    merged = jnp.transpose(node_states, (1, 2, 0, 3)).reshape(head_count, inner, level_count * outer).astype(jnp.float32)
    projected = jnp.einsum('bthd,hdf->bthf', query_rows.astype(jnp.float32), merged, precision=lax.Precision.HIGHEST)
    projected = projected.reshape(projected.shape[:3] + (level_count, outer))
    scale_rows = jnp.transpose(level_weights, (0, 3, 2, 1)).astype(jnp.float32)[..., None]
    return lax.optimization_barrier(jnp.sum(projected * scale_rows, axis=3))

def reference(slab_query, slab_key, slab_value, slab_levels, norm_gain, user_query, user_key, user_value, user_levels, prefix_lengths):
    tree_depth = N_SEQ.bit_length() - 1
    slab_queries = slab_query.reshape(N_SEQ, TOK_DEV, HEADS, HD)
    slab_keys = slab_key.reshape(N_SEQ, TOK_DEV, HEADS, HD)
    slab_values = slab_value.reshape(N_SEQ, TOK_DEV, HEADS, HD)
    block_states = jnp.einsum('cthd,cthe->chde', slab_keys.astype(jnp.float32), slab_values.astype(jnp.float32))
    block_states = lax.optimization_barrier(block_states.astype(jnp.bfloat16)).astype(jnp.float32)
    tiers = [block_states]
    for level_index in range(tree_depth):
        paired = tiers[-1].reshape(-1, 2, HEADS, HD, HD)
        tiers.append(paired[:, 0] + paired[:, 1])

    def nodes_of(position):
        collected = []
        for level_index in range(tree_depth):
            shifted = jnp.right_shift(position, level_index)
            sibling = jnp.bitwise_xor(shifted, 1).astype(jnp.int32)
            chosen = tiers[level_index][sibling]
            upper = jnp.bitwise_and(shifted, 1)
            collected.append(jnp.where(upper == 1, chosen, jnp.zeros_like(chosen)))
        stacked = jnp.stack(collected)
        return lax.optimization_barrier(stacked.astype(jnp.bfloat16)).astype(jnp.float32)
    slab_weights = slab_levels.reshape(LEVELS, HEADS, N_SEQ, TOK_DEV).transpose(2, 0, 1, 3)

    def slab_block(packed):
        position, query_rows, key_rows, value_rows, weights = packed
        local = local_part(query_rows[None], key_rows[None], value_rows[None], weights[None, 0])
        prefix = read_prefix(query_rows[None], weights[None, 1:1 + tree_depth], nodes_of(position))
        return (local + prefix)[0]
    slab_total = lax.map(slab_block, (jnp.arange(N_SEQ, dtype=jnp.int32), slab_queries, slab_keys, slab_values, slab_weights))
    user_queries = user_query.reshape(USERS, SUF, HEADS, HD)
    user_keys = user_key.reshape(USERS, SUF, HEADS, HD)
    user_values = user_value.reshape(USERS, SUF, HEADS, HD)

    def user_block(packed):
        position, query_rows, key_rows, value_rows, weights = packed
        local = local_part(query_rows[None], key_rows[None], value_rows[None], weights[None, 0])
        prefix = read_prefix(query_rows[None], weights[None, 1:1 + tree_depth], nodes_of(position))
        prefix = lax.optimization_barrier(prefix.astype(jnp.bfloat16)).astype(jnp.float32)
        return (local + prefix)[0]
    user_total = lax.map(user_block, (prefix_lengths.astype(jnp.int32), user_queries, user_keys, user_values, user_levels))
    gain_rows = norm_gain.reshape(HEADS, HD).astype(jnp.float32)

    def finish_norm(total):
        square_sum = lax.optimization_barrier(jnp.sum(total * total, axis=(-2, -1)))
        root_mean = jnp.sqrt(square_sum / (HEADS * HD) + 1e-06)
        return (total / root_mean[..., None, None] * gain_rows).astype(jnp.bfloat16)
    slab_out = finish_norm(slab_total).reshape(TOKENS, HEADS * HD)
    user_out = finish_norm(user_total).reshape(USERS, SUF, HEADS * HD)
    return (slab_out, user_out)
```

```python
import functools
import heapq

import jax
import jax.numpy as jnp
from jax import lax
from jax.experimental import pallas as pl
from jax.experimental.pallas import tpu as pltpu
from jax.sharding import PartitionSpec as P

HEADS = 64
HD = 128
MESH = pl.DeviceIdType.MESH
F32 = jnp.float32
BF16 = jnp.bfloat16

UNITS = (
    (0, 128, "A", 0, 0),
    (128, 128, "A", 2, 1),
    (256, 64, "A", 3, 0),
    (320, 64, "B", 3, 1),
    (384, 128, "B", 1, 0),
)
HEAD_UNITS = ((0,), (1,), (2, 3), (4,))
LINK_KB_PER_US = 46.5
HOP_US = 1.7
ISSUE_AHEAD_US = 2.0
PIECE_US = 0.6


def reach(ring, plus):
    return (ring // 2, (ring - 1) // 2) if plus else ((ring - 1) // 2, ring // 2)


def forwards(nx, ny, unit, ex, ey):
    _, _, route, _, parity = UNITS[unit]
    result = []

    def along_x(plus):
        ahead, back = reach(nx, plus)
        if 0 <= ex < ahead:
            result.append(("x+", ex + 1, ey))
        if 0 <= -ex < back:
            result.append(("x-", ex - 1, ey))

    def along_y(plus):
        ahead, back = reach(ny, plus)
        if 0 <= ey < ahead:
            result.append(("y+", ex, ey + 1))
        if 0 <= -ey < back:
            result.append(("y-", ex, ey - 1))

    if route == "A":
        if ex == 0:
            along_y(parity % 2 == 0)
        along_x((parity + ey) % 2 == 0)
    else:
        if ey == 0:
            along_x(parity % 2 == 0)
        along_y((parity + ex) % 2 == 0)
    return result


def gather_order(nx, ny):
    def depth(unit, ex, ey):
        return max([1 + depth(unit, a, b) for _, a, b in forwards(nx, ny, unit, ex, ey)], default=0)

    waiting = {link: [] for link in ("x+", "x-", "y+", "y-")}
    free = dict.fromkeys(waiting, 0.0)
    arrival = {(unit, 0, 0): 0.0 for unit in range(len(UNITS))}
    events = [(0.0, unit, 0, 0) for unit in range(len(UNITS))]
    heapq.heapify(events)
    sends, now = [], 0.0
    while True:
        while events and events[0][0] <= now + 1e-9:
            time, unit, ex, ey = heapq.heappop(events)
            for link, a, b in forwards(nx, ny, unit, ex, ey):
                entry = (UNITS[unit][3], -depth(unit, a, b), time, unit, ex, ey, a, b)
                heapq.heappush(waiting[link], entry)
        for link, queue in waiting.items():
            if queue and free[link] <= now + 1e-9:
                _, _, time, unit, ex, ey, a, b = heapq.heappop(queue)
                free[link] = now + UNITS[unit][1] * 0.25 / LINK_KB_PER_US
                sends.append((max(time, now - ISSUE_AHEAD_US), len(sends), link, unit, (ex, ey), (a, b)))
                arrival[(unit, a, b)] = free[link] + HOP_US
                heapq.heappush(events, (arrival[(unit, a, b)], unit, a, b))
        later = [event[0] for event in events[:1]]
        later += [free[link] for link, queue in waiting.items() if queue]
        later = [time for time in later if time > now]
        if not later:
            return sorted(sends), arrival
        now = min(later)


def kernel(
    n_seq,
    n_head,
    prefix_hbm,
    slab_q,
    slab_k,
    slab_v,
    slab_w,
    gain_hbm,
    user_q,
    user_k,
    user_v,
    user_w,
    slab_out,
    user_out,
    prefix_ref,
    q_buf,
    k_buf,
    v_buf,
    slab_w_buf,
    user_w_buf,
    gain_buf,
    blocks,
    nodes,
    scaled,
    total,
    staged,
    square_send,
    square_recv,
    root_buf,
    in_sem,
    out_sem,
    send_sem,
    recv_sem,
    head_send_sem,
    head_recv_sem,
):
    pairs = user_q.shape[0]
    heads = q_buf.shape[2] // HD
    suffix = q_buf.shape[1] // 2
    rows = 2 * suffix
    depth = n_seq.bit_length() - 1
    nx = 1 << (depth // 2)
    ny = n_seq // nx
    me = lax.axis_index("seq")
    me_head = lax.axis_index("head")
    x, y = me // ny, lax.rem(me, ny)

    def block_at(dx, dy):
        return lax.rem(x + (dx + nx), nx) * ny + lax.rem(y + (dy + ny), ny)

    loads = [
        pltpu.make_async_copy(source, target, in_sem.at[index])
        for index, (source, target) in enumerate(
            (
                (slab_k, k_buf.at[pairs]),
                (slab_v, v_buf.at[pairs]),
                (slab_q, q_buf.at[pairs]),
                (slab_w, slab_w_buf),
                (prefix_hbm, prefix_ref),
                (user_w, user_w_buf),
                (user_q, q_buf.at[pl.ds(0, pairs)]),
                (user_k, k_buf.at[pl.ds(0, pairs)]),
                (user_v, v_buf.at[pl.ds(0, pairs)]),
                (gain_hbm, gain_buf),
            )
        )
    ]
    for load in loads:
        load.start()

    neighbours = {
        "x+": block_at(1, 0),
        "x-": block_at(-1, 0),
        "y+": block_at(0, 1),
        "y-": block_at(0, -1),
    }
    barrier = pltpu.get_barrier_semaphore()
    for step in range(1, n_head):
        pl.semaphore_signal(
            barrier,
            inc=1,
            device_id=(me, lax.rem(me_head + step, n_head)),
            device_id_type=MESH,
        )
    for link in neighbours:
        pl.semaphore_signal(
            barrier, inc=1, device_id=(neighbours[link], me_head), device_id_type=MESH
        )

    loads[0].wait()
    loads[1].wait()
    for head in range(heads):
        lanes = slice(head * HD, (head + 1) * HD)
        state = lax.dot_general(
            k_buf[pairs, :, lanes],
            v_buf[pairs, :, lanes],
            (((0,), (0,)), ((), ())),
            preferred_element_type=F32,
        )
        blocks[me, lanes, :] = state.astype(BF16)
    pl.semaphore_wait(barrier, n_head - 1 + len(neighbours))

    sends, arrival = gather_order(nx, ny)
    slots = {key: index for index, key in enumerate(sorted(arrival))}

    def piece_copy(key, slot, link):
        unit, ex, ey = key
        piece = blocks.at[block_at(-ex, -ey), pl.ds(UNITS[unit][0], UNITS[unit][1])]
        return pltpu.make_async_remote_copy(
            src_ref=piece,
            dst_ref=piece,
            send_sem=send_sem.at[slot],
            recv_sem=recv_sem.at[slot],
            device_id=(neighbours[link], me_head),
            device_id_type=MESH,
        )

    arrived = {(unit, 0, 0) for unit in range(len(UNITS))}

    def await_piece(key):
        if key not in arrived:
            arrived.add(key)
            piece_copy(key, slots[key], "x+").wait_recv()

    row_ids = lax.broadcasted_iota(jnp.int32, (rows, rows), 0)
    col_ids = lax.broadcasted_iota(jnp.int32, (rows, rows), 1)
    causal = col_ids <= row_ids
    same_user = (row_ids // suffix) == (col_ids // suffix)
    spread = (
        lax.broadcasted_iota(jnp.int32, (heads, heads * HD), 0)
        == lax.broadcasted_iota(jnp.int32, (heads, heads * HD), 1) // HD
    ).astype(BF16)

    def widen(weights):
        return lax.dot_general(
            weights, spread, (((0,), (0,)), ((), ())), preferred_element_type=F32
        )

    def scale_rows(pair, first, count, weights_at, position):
        queries = q_buf[pair, pl.ds(first, count), :].astype(F32)
        for level in range(1, depth + 1):
            bit = lax.rem(position >> (level - 1), 2).astype(F32)
            product = (queries * (widen(weights_at(level)) * bit)).astype(BF16)
            for head in range(heads):
                scaled[pair, head, pl.ds(first, count), (level - 1) * HD : level * HD] = product[
                    :, head * HD : (head + 1) * HD
                ]

    def scale_piece(pair):
        if pair == pairs:
            scale_rows(pair, 0, rows, lambda level: slab_w_buf[level], me)
        else:
            for half in range(2):
                user = 2 * pair + half
                scale_rows(
                    pair,
                    half * suffix,
                    suffix,
                    lambda level: user_w_buf[user, level],
                    prefix_ref[user],
                )

    def local_piece(pair):
        if pair == pairs:
            weights = widen(slab_w_buf[0])
            mask = causal
        else:
            weights = jnp.concatenate(
                [widen(user_w_buf[2 * pair + half, 0]) for half in range(2)], axis=0
            )
            mask = jnp.logical_and(causal, same_user)
        for head in range(heads):
            lanes = slice(head * HD, (head + 1) * HD)
            scores = lax.dot_general(
                q_buf[pair, :, lanes],
                k_buf[pair, :, lanes],
                (((1,), (1,)), ((), ())),
                preferred_element_type=F32,
            )
            scores = jnp.where(mask, scores, 0.0).astype(BF16)
            result = jnp.dot(scores, v_buf[pair, :, lanes], preferred_element_type=F32)
            total[pair, :, lanes] = result * weights[:, lanes]

    first_node = [0]
    for level in range(1, depth + 1):
        first_node.append(first_node[-1] + (n_seq >> level))

    def build_nodes(head):
        chunk = 16

        @pl.loop(0, HD // chunk)
        def _(part):
            start = pl.multiple_of(part * chunk, chunk)
            source = pl.ds(pl.multiple_of(head * HD + part * chunk, chunk), chunk)

            def tree(level, index):
                if level == 0:
                    value = blocks[index, source, :]
                    if index % 2 == 0:
                        nodes[head, first_node[0] + index // 2, pl.ds(start, chunk), :] = value
                    return value.astype(F32)
                value = tree(level - 1, 2 * index) + tree(level - 1, 2 * index + 1)
                if level < depth and index % 2 == 0:
                    nodes[head, first_node[level] + index // 2, pl.ds(start, chunk), :] = (
                        value.astype(BF16)
                    )
                return value

            tree(depth - 1, 0)
            rest = 1
            for level in range(depth - 2, -1, -1):
                rest = 2 * rest
                tree(level, rest)
                rest = rest + 1

    def read_rows(pair, head, first, count, position):
        states = jnp.concatenate(
            [
                nodes[head, first_node[level - 1] + (position >> level)]
                for level in range(1, depth + 1)
            ],
            axis=0,
        )
        return jnp.dot(
            scaled[pair, head, pl.ds(first, count), :], states, preferred_element_type=F32
        )

    def read_pair(pair, head):
        lanes = slice(head * HD, (head + 1) * HD)
        if pair is None:
            total[pairs, :, lanes] += read_rows(pairs, head, 0, rows, me)
        else:
            for half in range(2):
                first = half * suffix
                total[pair, pl.ds(first, suffix), lanes] += read_rows(
                    pair, head, first, suffix, prefix_ref[2 * pair + half]
                )

    def read_head(head):
        for unit in HEAD_UNITS[head]:
            for key in sorted(arrival):
                if key[0] == unit:
                    await_piece(key)
        build_nodes(head)
        read_pair(None, head)

        @pl.loop(0, pairs)
        def _(pair):
            read_pair(pair, head)

    timeline = [(time, 0, index, "send", index) for index, (time, *_) in enumerate(sends)]
    pieces = []
    for step in range(pairs + 1):
        pair = pairs - step
        pieces += [(scale_piece, pair), (local_piece, pair)]
    last_load = {pairs: 4}
    for index, piece in enumerate(pieces):
        timeline.append((0.3 + PIECE_US * index, 1, index, "piece", piece))
    work_end = 0.3 + PIECE_US * len(pieces)
    for head in range(heads):
        done = max(
            time for key, time in arrival.items() if key[0] in HEAD_UNITS[head]
        )
        timeline.append((max(done, work_end) + 0.1, 2, head, "head", head))
    loads_waited = 2
    copies = []
    for _, _, _, kind, item in sorted(timeline, key=lambda entry: entry[:3]):
        if kind == "send":
            _, _, link, unit, (ex, ey), (a, b) = sends[item]
            await_piece((unit, ex, ey))
            source = blocks.at[block_at(-ex, -ey), pl.ds(UNITS[unit][0], UNITS[unit][1])]
            slot = slots[(unit, a, b)]
            copy = pltpu.make_async_remote_copy(
                src_ref=source,
                dst_ref=source,
                send_sem=send_sem.at[slot],
                recv_sem=recv_sem.at[slot],
                device_id=(neighbours[link], me_head),
                device_id_type=MESH,
            )
            copy.start()
            copies.append(copy)
        elif kind == "piece":
            work, pair = item
            needed = last_load.get(pair, 9)
            while loads_waited < needed:
                loads[loads_waited].wait()
                loads_waited += 1
            work(pair)
        else:
            read_head(item)
    loads[9].wait()

    lane_ids = lax.broadcasted_iota(jnp.int32, (rows, HD), 1)
    squares = jnp.zeros((rows, HD), F32)
    for pair in range(pairs + 1):
        values = total[pair]
        values = values * values
        column = jnp.sum(values, axis=1, keepdims=True)
        squares = jnp.where(lane_ids == pair, column, squares)
    kept = square_send.shape[0]
    square_send[...] = squares.T[:kept]
    head_copies = []
    for step in sorted(range(1, n_head), key=lambda s: -min(s, n_head - s)):
        copy = pltpu.make_async_remote_copy(
            src_ref=square_send,
            dst_ref=square_recv.at[step],
            send_sem=head_send_sem.at[step],
            recv_sem=head_recv_sem.at[step],
            device_id=(me, lax.rem(me_head + step, n_head)),
            device_id_type=MESH,
        )
        copy.start()
        head_copies.append((step, copy))
    summed = square_send[...]
    for step, copy in reversed(head_copies):
        copy.wait_recv()
        summed = summed + square_recv[step]
    inverse = 1.0 / jnp.sqrt(summed * (1.0 / (HEADS * HD)) + 1e-6)
    root_buf[...] = jnp.concatenate([inverse, jnp.zeros((HD - kept, rows), F32)], axis=0).T

    gain = gain_buf[...].astype(F32).reshape(1, heads * HD)
    outs = []
    for pair in range(pairs, -1, -1):
        scale = root_buf[:, pair : pair + 1]
        staged[pair] = (total[pair] * scale * gain).astype(BF16)
        target = slab_out if pair == pairs else user_out.at[pair]
        out = pltpu.make_async_copy(staged.at[pair], target, out_sem.at[pair])
        out.start()
        outs.append(out)
    for copy in copies:
        copy.wait_send()
    for _, copy in head_copies:
        copy.wait_send()
    for out in outs:
        out.wait()


def local(
    slab_query,
    slab_key,
    slab_value,
    slab_levels,
    norm_gain,
    user_query,
    user_key,
    user_value,
    user_levels,
    prefix_lengths,
):
    n_seq, n_head = lax.axis_size("seq"), lax.axis_size("head")
    tokens, width = slab_query.shape
    users, suffix = user_query.shape[:2]
    heads = width // HD
    pairs = users // 2
    depth = n_seq.bit_length() - 1
    paired = (pairs, 2 * suffix, width)
    whole = pl.BlockSpec(memory_space=pl.ANY)
    slot_count = n_seq * len(UNITS)
    buffers = (pairs + 1, tokens, width)
    kept = -(-(pairs + 1) // 8) * 8
    slab_out, user_out = pl.pallas_call(
        functools.partial(kernel, n_seq, n_head),
        out_shape=(
            jax.ShapeDtypeStruct((tokens, width), BF16),
            jax.ShapeDtypeStruct(paired, BF16),
        ),
        in_specs=[whole] * 10,
        out_specs=(whole, whole),
        scratch_shapes=[
            pltpu.SMEM(prefix_lengths.shape, jnp.int32),
            pltpu.VMEM(buffers, BF16),
            pltpu.VMEM(buffers, BF16),
            pltpu.VMEM(buffers, BF16),
            pltpu.VMEM(slab_levels.shape, BF16),
            pltpu.VMEM(user_levels.shape, BF16),
            pltpu.VMEM(norm_gain.shape, BF16),
            pltpu.VMEM((n_seq, width, HD), BF16),
            pltpu.VMEM((heads, n_seq - 1, HD, HD), BF16),
            pltpu.VMEM((pairs + 1, heads, tokens, depth * HD), BF16),
            pltpu.VMEM(buffers, F32),
            pltpu.VMEM(buffers, BF16),
            pltpu.VMEM((kept, tokens), F32),
            pltpu.VMEM((n_head, kept, tokens), F32),
            pltpu.VMEM((tokens, HD), F32),
            pltpu.SemaphoreType.DMA((10,)),
            pltpu.SemaphoreType.DMA((pairs + 1,)),
            pltpu.SemaphoreType.DMA((slot_count,)),
            pltpu.SemaphoreType.DMA((slot_count,)),
            pltpu.SemaphoreType.DMA((n_head,)),
            pltpu.SemaphoreType.DMA((n_head,)),
        ],
        compiler_params=pltpu.CompilerParams(
            collective_id=0, has_side_effects=True, vmem_limit_bytes=50 * 1024 * 1024
        ),
    )(
        *(
            pltpu.with_memory_space_constraint(array, pltpu.HBM)
            for array in (
                prefix_lengths,
                slab_query,
                slab_key,
                slab_value,
                slab_levels,
                norm_gain,
                user_query.reshape(paired),
                user_key.reshape(paired),
                user_value.reshape(paired),
                user_levels,
            )
        ),
    )
    return slab_out, user_out.reshape(user_query.shape)


def solution(mesh):
    return jax.shard_map(
        local,
        mesh=mesh,
        in_specs=(
            P("seq", "head"),
            P("seq", "head"),
            P("seq", "head"),
            P(None, "head", "seq"),
            P("head"),
            P("seq", None, "head"),
            P("seq", None, "head"),
            P("seq", None, "head"),
            P("seq", None, "head", None),
            P("seq"),
        ),
        out_specs=(P("seq", "head"), P("seq", None, "head")),
        check_vma=False,
    )
```

```python
import functools
import heapq

import jax
import jax.numpy as jnp
from jax import lax
from jax.experimental import pallas as pl
from jax.experimental.pallas import tpu as pltpu
from jax.sharding import PartitionSpec as P

HEADS = 64
HD = 128
MESH = pl.DeviceIdType.MESH
F32 = jnp.float32
BF16 = jnp.bfloat16

UNITS = (
    (0, 128, "A", 0, 0),
    (128, 128, "A", 2, 1),
    (256, 48, "A", 3, 0),
    (304, 80, "B", 3, 1),
    (384, 128, "B", 1, 0),
)
HEAD_UNITS = ((0,), (1,), (2, 3), (4,))
LINKS = ("x+", "x-", "y+", "y-")
LINK_KB_PER_US = 46.5
HOP_US = 2.6
ISSUE_AHEAD_US = 0.5
PRIORITY_WEIGHT = 0.3
WORK_US = 0.4


def reach(ring, plus):
    return (ring // 2, (ring - 1) // 2) if plus else ((ring - 1) // 2, ring // 2)


def forwards(nx, ny, unit, ex, ey):
    _, _, route, _, parity = UNITS[unit]
    result = []

    def along_x(plus):
        ahead, back = reach(nx, plus)
        if 0 <= ex < ahead:
            result.append(("x+", ex + 1, ey))
        if 0 <= -ex < back:
            result.append(("x-", ex - 1, ey))

    def along_y(plus):
        ahead, back = reach(ny, plus)
        if 0 <= ey < ahead:
            result.append(("y+", ex, ey + 1))
        if 0 <= -ey < back:
            result.append(("y-", ex, ey - 1))

    if route == "A":
        if ex == 0:
            along_y(parity % 2 == 0)
        along_x((parity + ey) % 2 == 0)
    else:
        if ey == 0:
            along_x(parity % 2 == 0)
        along_y((parity + ex) % 2 == 0)
    return result


def plan_gather(nx, ny, work_count):
    def depth(key):
        return max([1 + depth((key[0], a, b)) for _, a, b in forwards(nx, ny, *key)], default=0)

    def send_us(unit):
        return UNITS[unit][1] * 0.25 / LINK_KB_PER_US

    own = [(unit, 0, 0) for unit in range(len(UNITS))]
    waiting = {link: [] for link in LINKS}
    free = dict.fromkeys(LINKS, 0.0)
    events = [(0.0, key) for key in own]
    sends, now = [], 0.0
    while True:
        while events and events[0][0] <= now + 1e-9:
            time, key = heapq.heappop(events)
            for link, a, b in forwards(nx, ny, *key):
                target = (key[0], a, b)
                rank = UNITS[key[0]][3] * PRIORITY_WEIGHT - depth(target)
                heapq.heappush(waiting[link], (rank, time, key, target))
        for link, queue in waiting.items():
            if queue and free[link] <= now + 1e-9:
                _, time, key, target = heapq.heappop(queue)
                free[link] = now + send_us(key[0])
                heapq.heappush(events, (free[link] + HOP_US, target))
                sends.append((max(time, now - ISSUE_AHEAD_US), now, link, key, target))
        later = [event[0] for event in events[:1]]
        later += [free[link] for link, queue in waiting.items() if queue]
        later = [time for time in later if time > now + 1e-9]
        if not later:
            break
        now = min(later)

    arrival = dict.fromkeys(own, 0.0)
    free = dict.fromkeys(LINKS, 0.0)
    steps, now, work = [], 0.0, 0
    for _, _, link, key, target in sorted(sends):
        while work < work_count and arrival[key] - now > 0.6 * WORK_US:
            steps.append(("work", work))
            work, now = work + 1, now + WORK_US
        now = max(now, arrival[key])
        free[link] = max(now, free[link]) + send_us(key[0])
        arrival[target] = free[link] + HOP_US
        steps.append(("send", (link, key, target)))
    steps += [("work", index) for index in range(work, work_count)]
    complete = [
        max(time for key, time in arrival.items() if key[0] in units) for units in HEAD_UNITS
    ]
    order = sorted(range(len(HEAD_UNITS)), key=lambda head: complete[head])
    return steps, order, sorted(arrival)


def kernel(
    n_seq,
    n_head,
    prefix_hbm,
    slab_q,
    slab_k,
    slab_v,
    slab_w,
    gain_hbm,
    user_q,
    user_k,
    user_v,
    user_w,
    slab_out,
    user_out,
    prefix_ref,
    q_buf,
    k_buf,
    v_buf,
    slab_w_buf,
    user_w_buf,
    gain_buf,
    blocks,
    nodes,
    scaled,
    total,
    square_send,
    square_recv,
    in_sem,
    send_sem,
    recv_sem,
    head_send_sem,
    head_recv_sem,
):
    pairs = user_q.shape[0]
    width = q_buf.shape[2]
    heads = width // HD
    suffix = q_buf.shape[1] // 2
    rows = 2 * suffix
    depth = n_seq.bit_length() - 1
    nx = 1 << (depth // 2)
    ny = n_seq // nx
    me = lax.axis_index("seq")
    me_head = lax.axis_index("head")
    x, y = me // ny, lax.rem(me, ny)

    def block_at(dx, dy):
        return lax.rem(x + (dx + nx), nx) * ny + lax.rem(y + (dy + ny), ny)

    loads = [
        pltpu.make_async_copy(source, target, in_sem.at[index])
        for index, (source, target) in enumerate(
            (
                (slab_k, k_buf.at[pairs]),
                (slab_v, v_buf.at[pairs]),
                (slab_q, q_buf.at[pairs]),
                (slab_w, slab_w_buf),
                (prefix_hbm, prefix_ref),
                (user_w, user_w_buf),
                (user_q, q_buf.at[pl.ds(0, pairs)]),
                (user_k, k_buf.at[pl.ds(0, pairs)]),
                (user_v, v_buf.at[pl.ds(0, pairs)]),
                (gain_hbm, gain_buf),
            )
        )
    ]
    for load in loads[:2]:
        load.start()

    neighbours = {
        "x+": block_at(1, 0),
        "x-": block_at(-1, 0),
        "y+": block_at(0, 1),
        "y-": block_at(0, -1),
    }
    barrier = pltpu.get_barrier_semaphore()
    for step in range(1, n_head):
        pl.semaphore_signal(
            barrier,
            inc=1,
            device_id=(me, lax.rem(me_head + step, n_head)),
            device_id_type=MESH,
        )
    for link in neighbours:
        pl.semaphore_signal(
            barrier, inc=1, device_id=(neighbours[link], me_head), device_id_type=MESH
        )

    loads[0].wait()
    loads[1].wait()
    for head in range(heads):
        lanes = slice(head * HD, (head + 1) * HD)
        state = lax.dot_general(
            k_buf[pairs, :, lanes],
            v_buf[pairs, :, lanes],
            (((0,), (0,)), ((), ())),
            preferred_element_type=F32,
        )
        blocks[pl.ds(pl.multiple_of(me * width + head * HD, HD), HD), :] = state.astype(BF16)
    for load in loads[2:]:
        load.start()
    pl.semaphore_wait(barrier, n_head - 1 + len(neighbours))

    steps, head_order, pieces = plan_gather(nx, ny, 3 * (pairs + 1))
    relayed = [key for key in pieces if key[1:] != (0, 0) and forwards(nx, ny, *key)]
    kept_pieces = [key for key in pieces if not forwards(nx, ny, *key)]
    slots = {key: index for index, key in enumerate(relayed)}

    def piece_copy(link, key, target):
        unit, ex, ey = key
        start = pl.multiple_of(block_at(-ex, -ey) * width + UNITS[unit][0], 16)
        piece = blocks.at[pl.ds(start, UNITS[unit][1])]
        return pltpu.make_async_remote_copy(
            src_ref=piece,
            dst_ref=piece,
            send_sem=send_sem.at[LINKS.index(link)],
            recv_sem=recv_sem.at[slots.get(target, len(slots) + unit)],
            device_id=(neighbours[link], me_head),
            device_id_type=MESH,
        )

    def rows_copy(count, sem):
        rows_ref = blocks.at[pl.ds(0, count)]
        return pltpu.make_async_copy(rows_ref, rows_ref, sem)

    waited = set()

    def await_piece(key):
        if key in slots and key not in waited:
            waited.add(key)
            piece_copy("x+", key, key).wait_recv()

    row_ids = lax.broadcasted_iota(jnp.int32, (rows, rows), 0)
    col_ids = lax.broadcasted_iota(jnp.int32, (rows, rows), 1)
    causal = col_ids <= row_ids
    same_user = (row_ids // suffix) == (col_ids // suffix)
    spread = (
        lax.broadcasted_iota(jnp.int32, (heads, heads * HD), 0)
        == lax.broadcasted_iota(jnp.int32, (heads, heads * HD), 1) // HD
    ).astype(BF16)

    def widen(weights, lanes_of):
        return lax.dot_general(
            weights, lanes_of, (((0,), (0,)), ((), ())), preferred_element_type=F32
        )

    def scale_rows(pair, first, count, weights_at, position):
        queries = q_buf[pair, pl.ds(first, count), :].astype(F32)
        for level in range(1, depth + 1):
            bit = lax.rem(position >> (level - 1), 2).astype(F32)
            product = (queries * (widen(weights_at(level), spread) * bit)).astype(BF16)
            for head in range(heads):
                scaled[pair, head, pl.ds(first, count), (level - 1) * HD : level * HD] = product[
                    :, head * HD : (head + 1) * HD
                ]

    def scale_piece(pair):
        if pair == pairs:
            scale_rows(pair, 0, rows, lambda level: slab_w_buf[level], me)
        else:
            for half in range(2):
                user = 2 * pair + half
                scale_rows(
                    pair,
                    half * suffix,
                    suffix,
                    lambda level: user_w_buf[user, level],
                    prefix_ref[user],
                )

    def local_piece(pair, group):
        group_lanes = slice(group[0] * HD, (group[-1] + 1) * HD)
        if pair == pairs:
            weights = widen(slab_w_buf[0], spread[:, group_lanes])
            mask = causal
        else:
            weights = jnp.concatenate(
                [
                    widen(user_w_buf[2 * pair + half, 0], spread[:, group_lanes])
                    for half in range(2)
                ],
                axis=0,
            )
            mask = jnp.logical_and(causal, same_user)
        for index, head in enumerate(group):
            lanes = slice(head * HD, (head + 1) * HD)
            scores = lax.dot_general(
                q_buf[pair, :, lanes],
                k_buf[pair, :, lanes],
                (((1,), (1,)), ((), ())),
                preferred_element_type=F32,
            )
            scores = jnp.where(mask, scores, 0.0).astype(BF16)
            result = jnp.dot(scores, v_buf[pair, :, lanes], preferred_element_type=F32)
            total[pair, :, lanes] = result * weights[:, index * HD : (index + 1) * HD]

    first_node = [0]
    for level in range(1, depth + 1):
        first_node.append(first_node[-1] + (n_seq >> level))

    def build_nodes(head):
        chunk = 16

        @pl.loop(0, HD // chunk)
        def _(part):
            start = pl.multiple_of(part * chunk, chunk)

            def tree(level, index):
                if level == 0:
                    first = pl.multiple_of(index * width + head * HD + start, chunk)
                    value = blocks[pl.ds(first, chunk), :]
                    if index % 2 == 0:
                        nodes[head, first_node[0] + index // 2, pl.ds(start, chunk), :] = value
                    return value.astype(F32)
                value = tree(level - 1, 2 * index) + tree(level - 1, 2 * index + 1)
                if level < depth and index % 2 == 0:
                    nodes[head, first_node[level] + index // 2, pl.ds(start, chunk), :] = (
                        value.astype(BF16)
                    )
                return value

            tree(depth - 1, 0)
            rest = 1
            for level in range(depth - 2, -1, -1):
                rest = 2 * rest
                tree(level, rest)
                rest = rest + 1

    def read_rows(pair, head, first, count, position):
        states = jnp.concatenate(
            [
                nodes[head, first_node[level - 1] + (position >> level)]
                for level in range(1, depth + 1)
            ],
            axis=0,
        )
        return jnp.dot(
            scaled[pair, head, pl.ds(first, count), :], states, preferred_element_type=F32
        )

    def read_pair(pair, head):
        lanes = slice(head * HD, (head + 1) * HD)
        if pair is None:
            total[pairs, :, lanes] += read_rows(pairs, head, 0, rows, me)
        else:
            for half in range(2):
                first = half * suffix
                total[pair, pl.ds(first, suffix), lanes] += read_rows(
                    pair, head, first, suffix, prefix_ref[2 * pair + half]
                )

    work_items = []
    for pair in range(pairs, -1, -1):
        work_items.append(functools.partial(scale_piece, pair))
        for group in (range(heads // 2), range(heads // 2, heads)):
            work_items.append(functools.partial(local_piece, pair, group))

    loaded = False
    sent_rows = dict.fromkeys(LINKS, 0)
    for kind, item in steps:
        if kind == "work":
            for load in () if loaded else loads[2:]:
                load.wait()
            loaded = True
            work_items[item]()
        else:
            link, key, target = item
            await_piece(key)
            piece_copy(link, key, target).start()
            sent_rows[link] += UNITS[key[0]][1]
    for head in head_order:
        for unit in HEAD_UNITS[head]:
            for key in relayed:
                if key[0] == unit:
                    await_piece(key)
            kept_rows = UNITS[unit][1] * sum(key[0] == unit for key in kept_pieces)
            rows_copy(kept_rows, recv_sem.at[len(slots) + unit]).wait()
        build_nodes(head)
        read_pair(None, head)
        for pair in range(pairs):
            read_pair(pair, head)

    lane_ids = lax.broadcasted_iota(jnp.int32, (rows, HD), 1)
    squares = jnp.zeros((rows, HD), F32)
    for pair in range(pairs + 1):
        values = total[pair]
        values = values * values
        column = jnp.sum(values, axis=1, keepdims=True)
        squares = jnp.where(lane_ids == pair, column, squares)
    kept = square_send.shape[0]
    square_send[...] = squares.T[:kept]
    for step in sorted(range(1, n_head), key=lambda s: -min(s, n_head - s)):
        pltpu.make_async_remote_copy(
            src_ref=square_send.at[pl.ds(0, pairs + 1)],
            dst_ref=square_recv.at[step - 1, pl.ds(0, pairs + 1)],
            send_sem=head_send_sem,
            recv_sem=head_recv_sem,
            device_id=(me, lax.rem(me_head + step, n_head)),
            device_id_type=MESH,
        ).start()
    if n_head > 1:
        used = square_recv.at[:, pl.ds(0, pairs + 1)]
        pltpu.make_async_copy(used, used, head_recv_sem).wait()
    summed = square_send[...]
    for step in range(1, n_head):
        summed = summed + square_recv[step - 1]
    used_rows = lax.broadcasted_iota(jnp.int32, summed.shape, 0) <= pairs
    mean = jnp.where(used_rows, summed, 0.0) * (1.0 / (HEADS * HD))
    inverse = 1.0 / jnp.sqrt(mean + 1e-6)
    gain = gain_buf[...].astype(F32).reshape(1, width)
    roots = jnp.concatenate([inverse, jnp.zeros((HD - kept, rows), F32)], axis=0).T
    for pair in range(pairs, -1, -1):
        target = slab_out if pair == pairs else user_out.at[pair]
        target[...] = (total[pair] * roots[:, pair : pair + 1] * gain).astype(BF16)
    for link in LINKS:
        if sent_rows[link]:
            rows_copy(sent_rows[link], send_sem.at[LINKS.index(link)]).wait()
    if n_head > 1:
        pltpu.make_async_copy(used, used, head_send_sem).wait()


def local(
    slab_query,
    slab_key,
    slab_value,
    slab_levels,
    norm_gain,
    user_query,
    user_key,
    user_value,
    user_levels,
    prefix_lengths,
):
    n_seq, n_head = lax.axis_size("seq"), lax.axis_size("head")
    tokens, width = slab_query.shape
    users, suffix = user_query.shape[:2]
    heads = width // HD
    pairs = users // 2
    depth = n_seq.bit_length() - 1
    paired = (pairs, 2 * suffix, width)
    whole = pl.BlockSpec(memory_space=pl.ANY)
    nx = 1 << (depth // 2)
    pieces = plan_gather(nx, n_seq // nx, 0)[2]
    relayed = [key for key in pieces if key[1:] != (0, 0) and forwards(nx, n_seq // nx, *key)]
    recv_count = len(relayed) + len(UNITS)
    buffers = (pairs + 1, tokens, width)
    kept = -(-(pairs + 1) // 8) * 8
    slab_out, user_out = pl.pallas_call(
        functools.partial(kernel, n_seq, n_head),
        out_shape=(
            jax.ShapeDtypeStruct((tokens, width), BF16),
            jax.ShapeDtypeStruct(paired, BF16),
        ),
        in_specs=[whole] * 10,
        out_specs=(pl.BlockSpec(memory_space=pltpu.VMEM),) * 2,
        scratch_shapes=[
            pltpu.SMEM(prefix_lengths.shape, jnp.int32),
            pltpu.VMEM(buffers, BF16),
            pltpu.VMEM(buffers, BF16),
            pltpu.VMEM(buffers, BF16),
            pltpu.VMEM(slab_levels.shape, BF16),
            pltpu.VMEM(user_levels.shape, BF16),
            pltpu.VMEM(norm_gain.shape, BF16),
            pltpu.VMEM((n_seq * width, HD), BF16),
            pltpu.VMEM((heads, n_seq - 1, HD, HD), BF16),
            pltpu.VMEM((pairs + 1, heads, tokens, depth * HD), BF16),
            pltpu.VMEM(buffers, F32),
            pltpu.VMEM((kept, tokens), F32),
            pltpu.VMEM((max(n_head - 1, 1), kept, tokens), F32),
            pltpu.SemaphoreType.DMA((10,)),
            pltpu.SemaphoreType.DMA((len(LINKS),)),
            pltpu.SemaphoreType.DMA((recv_count,)),
            pltpu.SemaphoreType.DMA,
            pltpu.SemaphoreType.DMA,
        ],
        compiler_params=pltpu.CompilerParams(
            collective_id=0, has_side_effects=True, vmem_limit_bytes=50 * 1024 * 1024
        ),
    )(
        *(
            pltpu.with_memory_space_constraint(array, pltpu.HBM)
            for array in (
                prefix_lengths,
                slab_query,
                slab_key,
                slab_value,
                slab_levels,
                norm_gain,
                user_query.reshape(paired),
                user_key.reshape(paired),
                user_value.reshape(paired),
                user_levels,
            )
        ),
    )
    return slab_out, user_out.reshape(user_query.shape)


def solution(mesh):
    return jax.shard_map(
        local,
        mesh=mesh,
        in_specs=(
            P("seq", "head"),
            P("seq", "head"),
            P("seq", "head"),
            P(None, "head", "seq"),
            P("head"),
            P("seq", None, "head"),
            P("seq", None, "head"),
            P("seq", None, "head"),
            P("seq", None, "head", None),
            P("seq"),
        ),
        out_specs=(P("seq", "head"), P("seq", None, "head")),
        check_vma=False,
    )
```

```python
import functools
import heapq

import jax
import jax.numpy as jnp
from jax import lax
from jax.experimental import pallas as pl
from jax.experimental.pallas import tpu as pltpu
from jax.sharding import PartitionSpec as P

HEADS = 64
HD = 128
MESH = pl.DeviceIdType.MESH
F32 = jnp.float32
BF16 = jnp.bfloat16

UNITS = (
    (0, 128, "A", 0, 0),
    (128, 128, "A", 2, 1),
    (256, 48, "A", 3, 0),
    (304, 80, "B", 3, 1),
    (384, 128, "B", 1, 0),
)
HEAD_UNITS = ((0,), (1,), (2, 3), (4,))
LINKS = ("x+", "x-", "y+", "y-")
LINK_KB_PER_US = 46.5
HOP_US = 2.6
ISSUE_AHEAD_US = 0.5
PRIORITY_WEIGHT = 0.3
WORK_US = 0.3
WORK_GAP = 0.8
GREET_FROM_US = 10.0
GREET_EVERY_US = 3.0


def reach(ring, plus):
    return (ring // 2, (ring - 1) // 2) if plus else ((ring - 1) // 2, ring // 2)


def forwards(nx, ny, unit, ex, ey):
    _, _, route, _, parity = UNITS[unit]
    result = []

    def along_x(plus):
        ahead, back = reach(nx, plus)
        if 0 <= ex < ahead:
            result.append(("x+", ex + 1, ey))
        if 0 <= -ex < back:
            result.append(("x-", ex - 1, ey))

    def along_y(plus):
        ahead, back = reach(ny, plus)
        if 0 <= ey < ahead:
            result.append(("y+", ex, ey + 1))
        if 0 <= -ey < back:
            result.append(("y-", ex, ey - 1))

    if route == "A":
        if ex == 0:
            along_y(parity % 2 == 0)
        along_x((parity + ey) % 2 == 0)
    else:
        if ey == 0:
            along_x(parity % 2 == 0)
        along_y((parity + ex) % 2 == 0)
    return result


def plan_gather(nx, ny, work_count, rounds):
    def depth(key):
        return max([1 + depth((key[0], a, b)) for _, a, b in forwards(nx, ny, *key)], default=0)

    def send_us(unit):
        return UNITS[unit][1] * 0.25 / LINK_KB_PER_US

    own = [(unit, 0, 0) for unit in range(len(UNITS))]
    waiting = {link: [] for link in LINKS}
    free = dict.fromkeys(LINKS, 0.0)
    events = [(0.0, key) for key in own]
    sends, now = [], 0.0
    while True:
        while events and events[0][0] <= now + 1e-9:
            time, key = heapq.heappop(events)
            for link, a, b in forwards(nx, ny, *key):
                target = (key[0], a, b)
                rank = UNITS[key[0]][3] * PRIORITY_WEIGHT - depth(target)
                heapq.heappush(waiting[link], (rank, time, key, target))
        for link, queue in waiting.items():
            if queue and free[link] <= now + 1e-9:
                _, time, key, target = heapq.heappop(queue)
                free[link] = now + send_us(key[0])
                heapq.heappush(events, (free[link] + HOP_US, target))
                sends.append((max(time, now - ISSUE_AHEAD_US), now, link, key, target))
        later = [event[0] for event in events[:1]]
        later += [free[link] for link, queue in waiting.items() if queue]
        later = [time for time in later if time > now + 1e-9]
        if not later:
            break
        now = min(later)

    arrival = dict.fromkeys(own, 0.0)
    free = dict.fromkeys(LINKS, 0.0)
    steps, now, work, greetings = [], 0.0, 0, 0
    for _, _, link, key, target in sorted(sends):
        while work < work_count and arrival[key] - now > WORK_GAP * WORK_US:
            steps.append(("work", work))
            work, now = work + 1, now + WORK_US
        now = max(now, arrival[key])
        if greetings < rounds and now > GREET_FROM_US + GREET_EVERY_US * greetings:
            steps.append(("greet", greetings))
            greetings += 1
        free[link] = max(now, free[link]) + send_us(key[0])
        arrival[target] = free[link] + HOP_US
        steps.append(("send", (link, key, target)))
    steps += [("work", index) for index in range(work, work_count)]
    steps += [("greet", index) for index in range(greetings, rounds)]
    complete = [
        max(time for key, time in arrival.items() if key[0] in units) for units in HEAD_UNITS
    ]
    order = sorted(range(len(HEAD_UNITS)), key=lambda head: complete[head])
    return steps, order, sorted(arrival)


def kernel(
    n_seq,
    n_head,
    prefix_hbm,
    slab_q,
    slab_k,
    slab_v,
    slab_w,
    gain_hbm,
    user_q,
    user_k,
    user_v,
    user_w,
    slab_out,
    user_out,
    prefix_ref,
    q_buf,
    k_buf,
    v_buf,
    slab_w_buf,
    user_w_buf,
    gain_buf,
    blocks,
    nodes,
    scaled,
    total,
    square_send,
    square_recv,
    in_sem,
    send_sem,
    recv_sem,
    head_send_sem,
    head_recv_sem,
    greet_sem,
):
    pairs = user_q.shape[0]
    width = q_buf.shape[2]
    heads = width // HD
    suffix = q_buf.shape[1] // 2
    rows = 2 * suffix
    depth = n_seq.bit_length() - 1
    nx = 1 << (depth // 2)
    ny = n_seq // nx
    me = lax.axis_index("seq")
    me_head = lax.axis_index("head")
    x, y = me // ny, lax.rem(me, ny)

    def block_at(dx, dy):
        return lax.rem(x + (dx + nx), nx) * ny + lax.rem(y + (dy + ny), ny)

    loads = [
        pltpu.make_async_copy(source, target, in_sem.at[heads + index])
        for index, (source, target) in enumerate(
            (
                (slab_q, q_buf.at[pairs]),
                (slab_w, slab_w_buf),
                (prefix_hbm, prefix_ref),
                (user_w, user_w_buf),
                (user_q, q_buf.at[pl.ds(0, pairs)]),
                (user_k, k_buf.at[pl.ds(0, pairs)]),
                (user_v, v_buf.at[pl.ds(0, pairs)]),
                (gain_hbm, gain_buf),
            )
        )
    ]
    for head in range(heads):
        lanes = slice(head * HD, (head + 1) * HD)
        for source, target in ((slab_k, k_buf), (slab_v, v_buf)):
            pltpu.make_async_copy(
                source.at[:, lanes], target.at[pairs, :, lanes], in_sem.at[head]
            ).start()

    neighbours = {
        "x+": block_at(1, 0),
        "x-": block_at(-1, 0),
        "y+": block_at(0, 1),
        "y-": block_at(0, -1),
    }
    core, chip, chips = lax.rem(me_head, 2), me_head // 2, n_head // 2
    beside = [
        lax.rem(chip + step, chips) * 2 + core for step in sorted({1, chips - 1} - {0, chips})
    ]
    greeted = [(neighbours[link], me_head) for link in LINKS]
    greeted += [(me, head) for head in beside]
    if n_head > 1:
        greeted.append((me, me_head + 1 - 2 * core))
    barrier = pltpu.get_barrier_semaphore()
    for device in greeted:
        pl.semaphore_signal(barrier, inc=1, device_id=device, device_id_type=MESH)

    def greet(index):
        for head in beside:
            pl.semaphore_signal(
                greet_sem.at[index], inc=1, device_id=(me, head), device_id_type=MESH
            )

    for load in loads:
        load.start()
    pl.semaphore_wait(barrier, len(greeted))
    rounds = chips // 2
    if rounds:
        greet(0)

    steps, head_order, pieces = plan_gather(nx, ny, (heads + 2) * (pairs + 1), rounds)
    relayed = [key for key in pieces if key[1:] != (0, 0) and forwards(nx, ny, *key)]
    kept_pieces = [key for key in pieces if not forwards(nx, ny, *key)]
    slots = {key: index for index, key in enumerate(relayed)}

    def piece_copy(link, key, target):
        unit, ex, ey = key
        start = pl.multiple_of(block_at(-ex, -ey) * width + UNITS[unit][0], 16)
        piece = blocks.at[pl.ds(start, UNITS[unit][1])]
        return pltpu.make_async_remote_copy(
            src_ref=piece,
            dst_ref=piece,
            send_sem=send_sem.at[LINKS.index(link)],
            recv_sem=recv_sem.at[slots.get(target, len(slots) + unit)],
            device_id=(neighbours[link], me_head),
            device_id_type=MESH,
        )

    def rows_copy(count, sem):
        rows_ref = blocks.at[pl.ds(0, count)]
        return pltpu.make_async_copy(rows_ref, rows_ref, sem)

    waited = set()

    def await_piece(key):
        if key in slots and key not in waited:
            waited.add(key)
            piece_copy("x+", key, key).wait_recv()

    row_ids = lax.broadcasted_iota(jnp.int32, (rows, rows), 0)
    col_ids = lax.broadcasted_iota(jnp.int32, (rows, rows), 1)
    causal = col_ids <= row_ids
    same_user = (row_ids // suffix) == (col_ids // suffix)
    spread = (
        lax.broadcasted_iota(jnp.int32, (heads, heads * HD), 0)
        == lax.broadcasted_iota(jnp.int32, (heads, heads * HD), 1) // HD
    ).astype(BF16)

    def widen(weights, lanes_of):
        return lax.dot_general(
            weights, lanes_of, (((0,), (0,)), ((), ())), preferred_element_type=F32
        )

    def scale_rows(pair, first, count, weights_at, position):
        queries = q_buf[pair, pl.ds(first, count), :].astype(F32)
        for level in range(1, depth + 1):
            bit = lax.rem(position >> (level - 1), 2).astype(F32)
            product = (queries * (widen(weights_at(level), spread) * bit)).astype(BF16)
            for head in range(heads):
                scaled[pair, head, pl.ds(first, count), (level - 1) * HD : level * HD] = product[
                    :, head * HD : (head + 1) * HD
                ]

    def scale_piece(pair, half):
        first = half * suffix
        if pair == pairs:
            tokens = slice(first, first + suffix)
            scale_rows(pair, first, suffix, lambda level: slab_w_buf[level, :, tokens], me)
        else:
            user = 2 * pair + half
            scale_rows(
                pair, first, suffix, lambda level: user_w_buf[user, level], prefix_ref[user]
            )

    def local_piece(pair, group):
        group_lanes = slice(group[0] * HD, (group[-1] + 1) * HD)
        if pair == pairs:
            weights = widen(slab_w_buf[0], spread[:, group_lanes])
            mask = causal
        else:
            weights = jnp.concatenate(
                [
                    widen(user_w_buf[2 * pair + half, 0], spread[:, group_lanes])
                    for half in range(2)
                ],
                axis=0,
            )
            mask = jnp.logical_and(causal, same_user)
        for index, head in enumerate(group):
            lanes = slice(head * HD, (head + 1) * HD)
            scores = lax.dot_general(
                q_buf[pair, :, lanes],
                k_buf[pair, :, lanes],
                (((1,), (1,)), ((), ())),
                preferred_element_type=F32,
            )
            scores = jnp.where(mask, scores, 0.0).astype(BF16)
            result = jnp.dot(scores, v_buf[pair, :, lanes], preferred_element_type=F32)
            total[pair, :, lanes] = result * weights[:, index * HD : (index + 1) * HD]

    first_node = [0]
    for level in range(1, depth + 1):
        first_node.append(first_node[-1] + (n_seq >> level))

    def build_nodes(head):
        chunk = 16

        @pl.loop(0, HD // chunk)
        def _(part):
            start = pl.multiple_of(part * chunk, chunk)

            def tree(level, index):
                if level == 0:
                    first = pl.multiple_of(index * width + head * HD + start, chunk)
                    value = blocks[pl.ds(first, chunk), :]
                    if index % 2 == 0:
                        nodes[head, first_node[0] + index // 2, pl.ds(start, chunk), :] = value
                    return value.astype(F32)
                value = tree(level - 1, 2 * index) + tree(level - 1, 2 * index + 1)
                if level < depth and index % 2 == 0:
                    nodes[head, first_node[level] + index // 2, pl.ds(start, chunk), :] = (
                        value.astype(BF16)
                    )
                return value

            tree(depth - 1, 0)
            rest = 1
            for level in range(depth - 2, -1, -1):
                rest = 2 * rest
                tree(level, rest)
                rest = rest + 1

    def read_rows(pair, head, first, count, position):
        states = jnp.concatenate(
            [
                nodes[head, first_node[level - 1] + (position >> level)]
                for level in range(1, depth + 1)
            ],
            axis=0,
        )
        return jnp.dot(
            scaled[pair, head, pl.ds(first, count), :], states, preferred_element_type=F32
        )

    def read_pair(pair, head):
        lanes = slice(head * HD, (head + 1) * HD)
        if pair == pairs:
            total[pairs, :, lanes] += read_rows(pairs, head, 0, rows, me)
        else:
            for half in range(2):
                first = half * suffix
                total[pair, pl.ds(first, suffix), lanes] += read_rows(
                    pair, head, first, suffix, prefix_ref[2 * pair + half]
                )

    work_items = []
    for pair in range(pairs, -1, -1):
        for half in range(2):
            work_items.append(functools.partial(scale_piece, pair, half))
        for head in range(heads):
            work_items.append(functools.partial(local_piece, pair, (head,)))

    for head in range(heads):
        rows_copy(2 * rows, in_sem.at[head]).wait()
    for head in range(heads):
        lanes = slice(head * HD, (head + 1) * HD)
        state = lax.dot_general(
            k_buf[pairs, :, lanes],
            v_buf[pairs, :, lanes],
            (((0,), (0,)), ((), ())),
            preferred_element_type=F32,
        )
        blocks[pl.ds(pl.multiple_of(me * width + head * HD, HD), HD), :] = state.astype(BF16)
    loaded = False
    sent_rows = dict.fromkeys(LINKS, 0)
    for kind, item in steps:
        if kind == "work":
            for load in () if loaded else loads:
                load.wait()
            loaded = True
            work_items[item]()
        elif kind == "greet":
            pl.semaphore_wait(greet_sem.at[item], len(beside))
            if item + 1 < rounds:
                greet(item + 1)
        else:
            link, key, target = item
            await_piece(key)
            piece_copy(link, key, target).start()
            sent_rows[link] += UNITS[key[0]][1]
    lane_ids = lax.broadcasted_iota(jnp.int32, (rows, HD), 1)
    squares = jnp.zeros((rows, HD), F32)
    for head in head_order:
        for unit in HEAD_UNITS[head]:
            for key in relayed:
                if key[0] == unit:
                    await_piece(key)
            kept_rows = UNITS[unit][1] * sum(key[0] == unit for key in kept_pieces)
            rows_copy(kept_rows, recv_sem.at[len(slots) + unit]).wait()
        build_nodes(head)
        for pair in range(pairs, -1, -1):
            read_pair(pair, head)
            if head == head_order[-1]:
                values = total[pair]
                column = jnp.sum(values * values, axis=1, keepdims=True)
                squares = jnp.where(lane_ids == pair, column, squares)

    kept = square_send.shape[0]
    square_send[...] = squares.T[:kept]
    for step in sorted(range(1, n_head), key=lambda s: -min(s, n_head - s)):
        pltpu.make_async_remote_copy(
            src_ref=square_send.at[pl.ds(0, pairs + 1)],
            dst_ref=square_recv.at[step - 1, pl.ds(0, pairs + 1)],
            send_sem=head_send_sem,
            recv_sem=head_recv_sem,
            device_id=(me, lax.rem(me_head + step, n_head)),
            device_id_type=MESH,
        ).start()
    if n_head > 1:
        used = square_recv.at[:, pl.ds(0, pairs + 1)]
        pltpu.make_async_copy(used, used, head_recv_sem).wait()
    summed = square_send[...]
    for step in range(1, n_head):
        summed = summed + square_recv[step - 1]
    used_rows = lax.broadcasted_iota(jnp.int32, summed.shape, 0) <= pairs
    mean = jnp.where(used_rows, summed, 0.0) * (1.0 / (HEADS * HD))
    inverse = 1.0 / jnp.sqrt(mean + 1e-6)
    gain = gain_buf[...].astype(F32).reshape(1, width)
    roots = jnp.concatenate([inverse, jnp.zeros((HD - kept, rows), F32)], axis=0).T
    for pair in range(pairs, -1, -1):
        target = slab_out if pair == pairs else user_out.at[pair]
        target[...] = (total[pair] * roots[:, pair : pair + 1] * gain).astype(BF16)
    for link in LINKS:
        if sent_rows[link]:
            rows_copy(sent_rows[link], send_sem.at[LINKS.index(link)]).wait()
    if n_head > 1:
        pltpu.make_async_copy(used, used, head_send_sem).wait()


def local(
    slab_query,
    slab_key,
    slab_value,
    slab_levels,
    norm_gain,
    user_query,
    user_key,
    user_value,
    user_levels,
    prefix_lengths,
):
    n_seq, n_head = lax.axis_size("seq"), lax.axis_size("head")
    tokens, width = slab_query.shape
    users, suffix = user_query.shape[:2]
    heads = width // HD
    pairs = users // 2
    depth = n_seq.bit_length() - 1
    paired = (pairs, 2 * suffix, width)
    whole = pl.BlockSpec(memory_space=pl.ANY)
    nx = 1 << (depth // 2)
    pieces = plan_gather(nx, n_seq // nx, 0, 0)[2]
    relayed = [key for key in pieces if key[1:] != (0, 0) and forwards(nx, n_seq // nx, *key)]
    recv_count = len(relayed) + len(UNITS)
    buffers = (pairs + 1, tokens, width)
    kept = -(-(pairs + 1) // 8) * 8
    slab_out, user_out = pl.pallas_call(
        functools.partial(kernel, n_seq, n_head),
        out_shape=(
            jax.ShapeDtypeStruct((tokens, width), BF16),
            jax.ShapeDtypeStruct(paired, BF16),
        ),
        in_specs=[whole] * 10,
        out_specs=(pl.BlockSpec(memory_space=pltpu.VMEM),) * 2,
        scratch_shapes=[
            pltpu.SMEM(prefix_lengths.shape, jnp.int32),
            pltpu.VMEM(buffers, BF16),
            pltpu.VMEM(buffers, BF16),
            pltpu.VMEM(buffers, BF16),
            pltpu.VMEM(slab_levels.shape, BF16),
            pltpu.VMEM(user_levels.shape, BF16),
            pltpu.VMEM(norm_gain.shape, BF16),
            pltpu.VMEM((n_seq * width, HD), BF16),
            pltpu.VMEM((heads, n_seq - 1, HD, HD), BF16),
            pltpu.VMEM((pairs + 1, heads, tokens, depth * HD), BF16),
            pltpu.VMEM(buffers, F32),
            pltpu.VMEM((kept, tokens), F32),
            pltpu.VMEM((max(n_head - 1, 1), kept, tokens), F32),
            pltpu.SemaphoreType.DMA((heads + 8,)),
            pltpu.SemaphoreType.DMA((len(LINKS),)),
            pltpu.SemaphoreType.DMA((recv_count,)),
            pltpu.SemaphoreType.DMA,
            pltpu.SemaphoreType.DMA,
            pltpu.SemaphoreType.REGULAR((max(n_head // 4, 1),)),
        ],
        compiler_params=pltpu.CompilerParams(
            collective_id=0, has_side_effects=True, vmem_limit_bytes=50 * 1024 * 1024
        ),
    )(
        *(
            pltpu.with_memory_space_constraint(array, pltpu.HBM)
            for array in (
                prefix_lengths,
                slab_query,
                slab_key,
                slab_value,
                slab_levels,
                norm_gain,
                user_query.reshape(paired),
                user_key.reshape(paired),
                user_value.reshape(paired),
                user_levels,
            )
        ),
    )
    return slab_out, user_out.reshape(user_query.shape)


def solution(mesh):
    return jax.shard_map(
        local,
        mesh=mesh,
        in_specs=(
            P("seq", "head"),
            P("seq", "head"),
            P("seq", "head"),
            P(None, "head", "seq"),
            P("head"),
            P("seq", None, "head"),
            P("seq", None, "head"),
            P("seq", None, "head"),
            P("seq", None, "head", None),
            P("seq"),
        ),
        out_specs=(P("seq", "head"), P("seq", None, "head")),
        check_vma=False,
    )
```
